512 devices in a mesh: leaf: 8 (over x, core), grid: 64 (over y, z).
Axes of the slice: x: 4, y: 4, z: 16, core: 2. Of those that a mesh axis runs over, the one named last changes fastest.
Arguments:
- front_diag: float32 [8, 8192], P('leaf', 'grid'), may hold values from 1 to 4
- children: bfloat16 [16, 4096, 4096], P('leaf', 'grid'), may hold values from 0 to 1, as said below
- parent: int32 [16], replicated, may hold values from 0 to 7, as said below
- front_blocks: int32 [8], replicated, may hold values from 64 to 128
- child_blocks: int32 [16], replicated, may hold values from 32 to 64
- row_map: int32 [16, 64], replicated, may hold values from 0 to 127, as said below
Outputs:
- factor: bfloat16 [8, 8192, 8192], P('leaf', 'grid')
The draws below stay inside these ranges and needn't reach their ends.
Inputs may be any that keep to these rules, and one draw needn't show every extreme that they name: Children 2 l and 2 l + 1 belong to leaf index l; one of them has parent l and the other has parent l xor 1, so each front has exactly two children. Each row_map[c] holds 64 distinct increasing block numbers, all below front_blocks[parent[c]]; only its first child_blocks[c] entries are used. Each children[c] is symmetric.
All inputs are finite; a program needn't handle non-finite values.
Results may differ from the reference program's by a relative error of at most 0.003.
The reference program's roundings to bfloat16 on the way count: a program that leaves them out, or rounds other values in their place, can miss the bound.
Values may be sent and summed in bfloat16 or wider, within the bound.
No kernel may reach another device: no remote copies, remote signals or barrier semaphores. Data moves between devices by JAX's collectives and lax.ppermute only.
A program may use at most 64 MiB of HBM per device.

```python
import math
import jax
import jax.numpy as jnp
from jax import lax

F = 8192
CU = 4096
BLK = 64
PW = 256
PANELS = 3
FRONTS = 8
CHILDREN = 16
FRONT_BLOCKS = 128
CHILD_BLOCKS = 64


def shuffled(subkey):
    return jax.random.permutation(subkey, FRONT_BLOCKS)


def tree_tables(key):
    bits = jax.random.randint(jax.random.fold_in(key, 101), (FRONTS,), 0, 2)
    child_index = jnp.arange(CHILDREN, dtype=jnp.int32)
    home = child_index // 2
    parent = jnp.where(child_index % 2 == bits[home], home, jnp.bitwise_xor(home, 1)).astype(jnp.int32)
    front_blocks = jax.random.randint(jax.random.fold_in(key, 102), (FRONTS,), FRONT_BLOCKS // 2, FRONT_BLOCKS + 1)
    order = jax.random.permutation(jax.random.fold_in(key, 103), FRONTS)
    front_blocks = front_blocks.at[order[0]].set(FRONT_BLOCKS).at[order[1]].set(FRONT_BLOCKS // 2)
    child_blocks = jax.random.randint(jax.random.fold_in(key, 104), (CHILDREN,), CHILD_BLOCKS // 2, CHILD_BLOCKS + 1)
    second = jax.random.permutation(jax.random.fold_in(key, 105), CHILDREN)
    child_blocks = child_blocks.at[second[0]].set(CHILD_BLOCKS).at[second[1]].set(CHILD_BLOCKS // 2)
    subkeys = jax.random.split(jax.random.fold_in(key, 106), CHILDREN)
    scores = jax.vmap(shuffled)(subkeys)
    limit = front_blocks[parent][:, None]
    places = jnp.arange(FRONT_BLOCKS, dtype=jnp.int32)[None, :]
    ranked = jnp.where(places < limit, scores, FRONT_BLOCKS + places)
    forced = (places == 0) | (places == limit - 1)
    ranked = jnp.where(forced, -1, ranked)
    chosen = jnp.argsort(ranked, axis=1, stable=True)[:, :CHILD_BLOCKS]
    row_map = jnp.sort(chosen, axis=1).astype(jnp.int32)
    return (parent, front_blocks.astype(jnp.int32), child_blocks.astype(jnp.int32), row_map)


def draw_parent(key, part):
    return tree_tables(key)[0]


def draw_front_blocks(key, part):
    return tree_tables(key)[1]


def draw_child_blocks(key, part):
    return tree_tables(key)[2]


def draw_row_map(key, part):
    return tree_tables(key)[3]


def draw_children(key, part):
    reach = 0.6

    def kernel_child(child_key):
        coords = jax.random.uniform(child_key, (3, CU), jnp.float32)
        distance = jnp.zeros((CU, CU), jnp.float32)
        for direction in range(3):
            distance = distance + jnp.abs(coords[direction][:, None] - coords[direction][None, :])
        return jnp.exp(-distance / reach)
    child_keys = jax.random.split(jax.random.fold_in(key, 201), CHILDREN)
    return lax.map(kernel_child, child_keys).astype(jnp.bfloat16)


def levels(rng, extent, pieces, smallest, high):
    def one(dim, blocks):
        steps = jax.random.uniform(jax.random.fold_in(jax.random.fold_in(rng, 6), dim), (blocks,), jnp.float32, smallest / len(pieces), high / len(pieces))
        return jnp.repeat(jnp.exp(steps), extent[dim] // blocks).reshape((-1,) + (1,) * (len(extent) - dim - 1))

    factor_of = one(*pieces[0])
    for cut in pieces[1:]:
        factor_of = factor_of * one(*cut)
    return factor_of


def setup_inputs(seed: int = 0) -> dict:
    key_list = jax.random.split(jax.random.key(seed), 7)
    front_diag = jnp.clip(jnp.exp(math.log(4.0) - 1.3862944 * jax.random.uniform(key_list[0], (FRONTS, F), jnp.float32) ** levels(key_list[0], (FRONTS, F), ((0, 8), (1, 64)), -0.2, 0.2)), 1.0, 4.0)
    children = draw_children(jax.random.fold_in(key_list[6], 71), 0)
    parent = draw_parent(jax.random.fold_in(key_list[6], 71), 0)
    front_blocks = draw_front_blocks(jax.random.fold_in(key_list[6], 71), 0)
    child_blocks = draw_child_blocks(jax.random.fold_in(key_list[6], 71), 0)
    row_map = draw_row_map(jax.random.fold_in(key_list[6], 71), 0)
    return {"front_diag": front_diag, "children": children, "parent": parent, "front_blocks": front_blocks, "child_blocks": child_blocks, "row_map": row_map}


def pivot_parts(pivot_block):
    pivot_factor = jnp.linalg.cholesky(pivot_block)
    identity = jnp.eye(pivot_block.shape[0], dtype=pivot_block.dtype)
    pivot_inverse = jax.scipy.linalg.solve_triangular(pivot_factor, identity, lower=True)
    return (pivot_factor, pivot_inverse)

def assemble(front_index, front_diag, children, parent, front_blocks, child_blocks, row_map):
    matrix = jnp.zeros((F, F), jnp.float32)
    child_ids = jnp.nonzero(parent == front_index, size=2)[0]
    for slot in range(2):
        child_index = child_ids[slot]
        update_block = children[child_index].astype(jnp.float32)
        live = (jnp.arange(CU) // BLK < child_blocks[child_index]).astype(jnp.float32)
        update_block = update_block * live[:, None] * live[None, :]
        positions = (row_map[child_index][:, None] * BLK + jnp.arange(BLK)[None, :]).reshape(-1)
        matrix = matrix.at[positions[:, None], positions[None, :]].add(update_block)
    line = jnp.arange(F)
    active = front_blocks[front_index] * BLK
    on_diag = line[:, None] == line[None, :]
    matrix = matrix + jnp.where(on_diag, front_diag[front_index][:, None], jnp.float32(0.0))
    padding = (line[:, None] >= active) | (line[None, :] >= active)
    identity_part = jnp.where(on_diag, jnp.float32(1.0), jnp.float32(0.0))
    matrix = jnp.where(padding, identity_part, matrix)
    return matrix.astype(jnp.bfloat16)

def factor_front(matrix):
    for step in range(PANELS):
        left_edge = step * PW
        right_edge = left_edge + PW
        pivot_block = matrix[left_edge:right_edge, left_edge:right_edge].astype(jnp.float32)
        pivot_factor, pivot_inverse = pivot_parts(pivot_block)
        below = jnp.dot(matrix[right_edge:, left_edge:right_edge].astype(jnp.float32), pivot_inverse.T, precision=lax.Precision.HIGHEST)
        upper_zero = jnp.zeros((left_edge, PW), jnp.float32)
        panel_cols = jnp.concatenate([upper_zero, pivot_factor, below], 0).astype(jnp.bfloat16)
        lower_panel = panel_cols[right_edge:]
        trailing = matrix[right_edge:, right_edge:].astype(jnp.float32) - jnp.dot(lower_panel.astype(jnp.float32), lower_panel.T.astype(jnp.float32), preferred_element_type=jnp.float32)
        matrix = matrix.at[right_edge:, right_edge:].set(trailing.astype(jnp.bfloat16))
        matrix = matrix.at[:right_edge, right_edge:].set(jnp.zeros((right_edge, F - right_edge), jnp.bfloat16))
        matrix = matrix.at[:, left_edge:right_edge].set(panel_cols)
    return matrix

def reference(front_diag, children, parent, front_blocks, child_blocks, row_map):

    def one_front(front_index):
        assembled = assemble(front_index, front_diag, children, parent, front_blocks, child_blocks, row_map)
        return factor_front(assembled)
    return lax.map(one_front, jnp.arange(FRONTS, dtype=jnp.int32))
```

```python
import jax
import jax.numpy as jnp
from jax import lax
from jax.experimental import pallas as pl
from jax.experimental.pallas import tpu as pltpu
from jax.sharding import PartitionSpec as P

BLK = 64
PW = 256
PANELS = 3
TOP = PW * PANELS
ROWS = 128
SENT = 144
LEAF = 32
CHUNK = 1024
F32 = jnp.float32
BF16 = jnp.bfloat16
VMEM_LIMIT = 56 * 1024 * 1024


def swapped(value):
    pairs = [(source, source ^ 1) for source in range(lax.axis_size("leaf"))]
    return lax.ppermute(value, "leaf", pairs)


def split3(value):
    high = value.astype(BF16)
    rest = value - high.astype(F32)
    middle = rest.astype(BF16)
    low = (rest - middle.astype(F32)).astype(BF16)
    return high, middle, low


def dot_nt(left, right):
    return lax.dot_general(left, right, (((1,), (1,)), ((), ())), preferred_element_type=F32)


def rounded(value):
    return value.astype(BF16).astype(F32)


def pack_kernel(table, pick, children, arrived, diag, send, panel):
    lanes = lax.broadcasted_iota(jnp.int32, (BLK, 2 * BLK), 1)

    def half(child, source, slot, side):
        block = table[slot * 128 + source]
        index = jnp.maximum(block, 0)
        start = pl.multiple_of((index // 2) * 128, 128)
        tile = child(pl.ds(start, 128)).astype(F32)
        turned = pltpu.roll(tile, BLK, 1)
        tile = jnp.where(index % 2 == side, tile, turned)
        return jnp.where(block >= 0, tile, 0.0)

    def own(cols):
        return children[pick[0], :, cols]

    def far(cols):
        return arrived[:, cols]

    parts = split3(diag[...])
    tail = jnp.concatenate([part.astype(F32) for part in parts] + [jnp.zeros((13, 128), F32)], axis=0).astype(BF16)

    def step(pair, carry):
        for slot, child in ((0, own), (1, far)):
            tile = jnp.where(lanes < BLK, half(child, 2 * pair, slot, 0), half(child, 2 * pair + 1, slot, 1))
            tile = tile.astype(BF16)
            send[pair, slot * BLK : (slot + 1) * BLK, :] = tile

            @pl.when(pair < TOP // 128)
            def _():
                panel[slot * BLK : (slot + 1) * BLK, pl.ds(pl.multiple_of(pair * 128, 128), 128)] = tile

        send[pair, 2 * BLK : SENT, :] = tail
        return carry

    lax.fori_loop(0, send.shape[0], step, 0)


def pivot(work):
    row = lax.broadcasted_iota(jnp.int32, (LEAF, 1), 0)
    col = lax.broadcasted_iota(jnp.int32, (LEAF, PW), 1)
    for base in range(0, PW, LEAF):
        left = work[base : base + LEAF, :PW]
        right = work[base : base + LEAF, PW:]
        for j in range(0, LEAF, 2):
            c0 = left[:, base + j : base + j + 1]
            c1 = left[:, base + j + 1 : base + j + 2]
            a = c0[j : j + 1]
            b = c0[j + 1 : j + 2]
            c = c1[j + 1 : j + 2]
            scale = 1.0 / (a * c - b * b)
            below = row > j + 1
            ratio = b / a
            m0 = jnp.where(below, (c0 * c - c1 * b) * scale, jnp.where(row == j + 1, ratio, 0.0))
            m1 = jnp.where(below, (c1 * a - c0 * b) * scale, 0.0)
            l0, l1 = left[j : j + 1], left[j + 1 : j + 2]
            r0, r1 = right[j : j + 1], right[j + 1 : j + 2]
            left = left - (m0 * l0 + m1 * l1)
            right = right - (m0 * r0 + m1 * r1)
        pivots = jnp.sum(jnp.where(col == row + base, left, 0.0), axis=1, keepdims=True)
        unit = lax.rsqrt(pivots)
        unit = unit * (1.5 - 0.5 * pivots * unit * unit)
        upper = jnp.where(col >= row + base, left * unit, 0.0)
        right = right * unit
        work[base : base + LEAF, :PW] = upper
        work[base : base + LEAF, PW:] = right
        if base + LEAF < PW:
            beyond = upper[:, base + LEAF :].T
            both = jnp.concatenate([upper, right], axis=1)
            product = lax.dot_general(
                beyond, both, (((1,), (0,)), ((), ())), preferred_element_type=F32, precision=lax.Precision.HIGHEST
            )
            work[base + LEAF :, :] = work[base + LEAF :, :] - product


def top_kernel(table, gathered, diag, inverse, factor, matrix, work):
    count = TOP // BLK
    for block in range(count):
        total = jnp.zeros((BLK, TOP), F32)
        for slot in range(2):
            source = table[slot * 128 + block]
            rows = gathered[jnp.maximum(source, 0), slot * BLK : (slot + 1) * BLK, :].astype(F32)
            total = total + jnp.where(source >= 0, rows, 0.0)
        on = lax.broadcasted_iota(jnp.int32, (BLK, TOP), 0) + block * BLK == lax.broadcasted_iota(jnp.int32, (BLK, TOP), 1)
        matrix[block * BLK : (block + 1) * BLK, :] = rounded(total + jnp.where(on, diag[...], 0.0))
    factor[...] = jnp.zeros_like(factor)
    for step in range(PANELS):
        a, e = step * PW, (step + 1) * PW
        work[:, :PW] = matrix[a:e, a:e]
        square = lax.broadcasted_iota(jnp.int32, (PW, PW), 0) == lax.broadcasted_iota(jnp.int32, (PW, PW), 1)
        work[:, PW:] = jnp.where(square, 1.0, 0.0)
        pivot(work)
        parts = split3(work[:, PW:])
        for index in range(3):
            inverse[step, index] = parts[index]
        factor[a:e, a:e] = work[:, :PW].T.astype(BF16)
        if e < TOP:
            below = matrix[e:, a:e].astype(BF16)
            solved = dot_nt(below, parts[0]) + (dot_nt(below, parts[1]) + dot_nt(below, parts[2]))
            solved = solved.astype(BF16)
            factor[e:, a:e] = solved
            matrix[e:, e:] = rounded(matrix[e:, e:] - dot_nt(solved, solved))


def front_kernel(table, place, gathered, received, diag, inverse, top, out, factor):
    device, active = place[0], place[1]
    blocks = CHUNK // BLK

    def solve(chunk, carry):
        first = chunk * blocks
        rows = []
        for block in range(blocks):
            total = jnp.zeros((BLK, TOP), F32)
            for slot in range(2):
                source = table[slot * 128 + first + block]
                part = gathered[jnp.maximum(source, 0), slot * BLK : (slot + 1) * BLK, :].astype(F32)
                total = total + jnp.where(source >= 0, part, 0.0)
            spot = pl.ds(pl.multiple_of((first + block) * BLK, BLK), BLK)
            factor[spot, :] = total.astype(BF16)
        spot = pl.ds(pl.multiple_of(chunk * CHUNK, CHUNK), CHUNK)
        for step in range(PANELS):
            a, e = step * PW, (step + 1) * PW
            panel = factor[spot, a:e]
            for before in range(step):
                b0, b1 = before * PW, (before + 1) * PW
                panel = (panel.astype(F32) - dot_nt(factor[spot, b0:b1], top[a:e, b0:b1])).astype(BF16)
            solved = dot_nt(panel, inverse[step, 0]) + (dot_nt(panel, inverse[step, 1]) + dot_nt(panel, inverse[step, 2]))
            factor[spot, a:e] = solved.astype(BF16)
        return carry

    lax.fori_loop(0, factor.shape[0] // CHUNK, solve, 0)
    factor[:TOP, :] = top[...]
    own = factor[pl.ds(pl.multiple_of(device * ROWS, ROWS), ROWS), :]
    cols = device * ROWS + lax.broadcasted_iota(jnp.int32, (BLK, ROWS), 1)

    def update(chunk, carry):
        first = chunk * blocks
        tiles = []
        for block in range(blocks):
            total = jnp.zeros((BLK, ROWS), F32)
            for slot in range(2):
                source = table[slot * 128 + first + block]
                part = received[jnp.maximum(source, 0), slot * BLK : (slot + 1) * BLK, :].astype(F32)
                total = total + jnp.where(source >= 0, part, 0.0)
            rows = (first + block) * BLK + lax.broadcasted_iota(jnp.int32, (BLK, ROWS), 0)
            on = rows == cols
            total = total + jnp.where(on, diag[...], 0.0)
            outside = (rows >= active) | (cols >= active)
            tiles.append(jnp.where(outside, jnp.where(on, 1.0, 0.0), total))
        tile = rounded(jnp.concatenate(tiles, axis=0))
        spot = pl.ds(pl.multiple_of(chunk * CHUNK, CHUNK), CHUNK)
        for step in range(PANELS):
            a, e = step * PW, (step + 1) * PW
            tile = rounded(tile - dot_nt(factor[spot, a:e], own[:, a:e]))
        tile = jnp.where(device < TOP // ROWS, 0.0, tile)
        out[:, pl.ds(pl.multiple_of(chunk * CHUNK, CHUNK), CHUNK)] = tile.T.astype(BF16)
        return carry

    lax.fori_loop(0, factor.shape[0] // CHUNK, update, 0)
    out[:, :TOP] = own


def body(front_diag, children, parent, front_blocks, child_blocks, row_map):
    leaf = lax.axis_index("leaf")
    grid = lax.axis_index("grid")
    devices = lax.axis_size("grid")
    front_order = front_diag.shape[1] * devices
    first_own = 2 * leaf
    first_far = 2 * jnp.bitwise_xor(leaf, 1)
    own_slot = jnp.where(parent[first_own] == leaf, 0, 1).astype(jnp.int32)
    far_slot = jnp.where(parent[first_far] == leaf, 0, 1).astype(jnp.int32)
    arrived = swapped(lax.dynamic_index_in_dim(children, 1 - own_slot, 0, keepdims=False))
    ids = jnp.stack([first_own + own_slot, first_far + far_slot])
    maps = row_map[ids]
    numbers = jnp.arange(maps.shape[1], dtype=jnp.int32)
    live = numbers[None, :] < child_blocks[ids][:, None]
    hit = (maps[:, :, None] == jnp.arange(front_order // BLK)[None, None, :]) & live[:, :, None]
    table = jnp.max(jnp.where(hit, numbers[None, :, None], -1), axis=1).reshape(-1)

    smem = pl.BlockSpec(memory_space=pltpu.SMEM)
    vmem = pl.BlockSpec(memory_space=pltpu.VMEM)
    params = pltpu.CompilerParams(vmem_limit_bytes=VMEM_LIMIT)
    send, panel = pl.pallas_call(
        pack_kernel,
        out_shape=(
            jax.ShapeDtypeStruct((devices, SENT, 128), BF16),
            jax.ShapeDtypeStruct((2 * BLK, TOP), BF16),
        ),
        in_specs=[smem, smem, vmem, vmem, vmem],
        out_specs=(vmem, vmem),
        compiler_params=params,
    )(table, own_slot.reshape(1), children, arrived, front_diag)
    gathered = lax.all_gather(panel, "grid", axis=0, tiled=False)
    received = lax.all_to_all(send, "grid", 0, 0, tiled=True)
    parts = received[: TOP // ROWS, 2 * BLK : 2 * BLK + 3, :].astype(F32)
    top_diag = (parts[:, 0] + parts[:, 1] + parts[:, 2]).reshape(1, TOP)
    inverse, top = pl.pallas_call(
        top_kernel,
        out_shape=(
            jax.ShapeDtypeStruct((PANELS, 3, PW, PW), BF16),
            jax.ShapeDtypeStruct((TOP, TOP), BF16),
        ),
        in_specs=[smem, vmem, vmem],
        out_specs=(vmem, vmem),
        scratch_shapes=[pltpu.VMEM((TOP, TOP), F32), pltpu.VMEM((PW, 2 * PW), F32)],
        compiler_params=params,
    )(table, gathered, top_diag)
    place = jnp.stack([grid, front_blocks[leaf] * BLK]).astype(jnp.int32)
    factor = pl.pallas_call(
        front_kernel,
        out_shape=jax.ShapeDtypeStruct((ROWS, front_order), BF16),
        in_specs=[smem, smem, vmem, vmem, vmem, vmem, vmem],
        out_specs=vmem,
        scratch_shapes=[pltpu.VMEM((front_order, TOP), BF16)],
        compiler_params=params,
    )(table, place, gathered, received, front_diag, inverse, top)
    return factor[None]


def solution(mesh):
    in_specs = (P("leaf", "grid"), P("leaf", "grid", None), P(), P(), P(), P())
    return jax.shard_map(body, mesh=mesh, in_specs=in_specs, out_specs=P("leaf", "grid", None), check_vma=False)
```

```python
import jax
import jax.numpy as jnp
from jax import lax
from jax.experimental import pallas as pl
from jax.experimental.pallas import tpu as pltpu
from jax.sharding import PartitionSpec as P

BLK = 64
PW = 256
PANELS = 3
TOP = PW * PANELS
ROWS = 128
SENT = 144
LEAF = 16
HALF = 128
CHUNK = 1024
F32 = jnp.float32
BF16 = jnp.bfloat16
VMEM_LIMIT = 56 * 1024 * 1024


def swapped(value):
    pairs = [(source, source ^ 1) for source in range(lax.axis_size("leaf"))]
    return lax.ppermute(value, "leaf", pairs)


def split3(value):
    high = value.astype(BF16)
    rest = value - high.astype(F32)
    middle = rest.astype(BF16)
    low = (rest - middle.astype(F32)).astype(BF16)
    return high, middle, low


def dot_nt(left, right):
    return lax.dot_general(left, right, (((1,), (1,)), ((), ())), preferred_element_type=F32)


def rounded(value):
    return value.astype(BF16).astype(F32)


def spread_tile(child, first, second):
    lanes = lax.broadcasted_iota(jnp.int32, (BLK, 2 * BLK), 1)

    def half(block, side):
        index = jnp.maximum(block, 0)
        tile = child(pl.ds(pl.multiple_of((index // 2) * 128, 128), 128)).astype(F32)
        tile = jnp.where(index % 2 == side, tile, pltpu.roll(tile, BLK, 1))
        return jnp.where(block >= 0, tile, 0.0)

    return jnp.where(lanes < BLK, half(first, 0), half(second, 1)).astype(BF16)


def panel_kernel(leaf, parent, counts, row_map, children, arrived, panel):
    own_slot = jnp.where(parent[2 * leaf[0]] == leaf[0], 0, 1)
    far_first = 2 * jnp.bitwise_xor(leaf[0], 1)
    far_slot = jnp.where(parent[far_first] == leaf[0], 0, 1)
    for slot, source, pick, child_id in (
        (0, children, own_slot, 2 * leaf[0] + own_slot),
        (1, arrived, far_slot, far_first + far_slot),
    ):
        places = [
            jnp.where(block < counts[child_id], row_map[child_id * 64 + block], -1) for block in range(TOP // BLK)
        ]

        def find(target):
            found = jnp.int32(-1)
            for block, place in enumerate(places):
                found = jnp.where(place == target, block, found)
            return found

        def child(cols):
            return source[pick, :, cols]

        for pair in range(TOP // 128):
            tile = spread_tile(child, find(2 * pair), find(2 * pair + 1))
            panel[slot * BLK : (slot + 1) * BLK, pair * 128 : (pair + 1) * 128] = tile


def pack_kernel(table, pick, children, arrived, diag, send):
    def own(cols):
        return children[pick[0], :, cols]

    def far(cols):
        return arrived[:, cols]

    parts = split3(diag[...])
    tail = jnp.concatenate([part.astype(F32) for part in parts] + [jnp.zeros((13, 128), F32)], axis=0).astype(BF16)

    def step(pair, carry):
        for slot, child in ((0, own), (1, far)):
            send[pair, slot * BLK : (slot + 1) * BLK, :] = spread_tile(
                child, table[slot * 128 + 2 * pair], table[slot * 128 + 2 * pair + 1]
            )
        send[pair, 2 * BLK : SENT, :] = tail
        return carry

    lax.fori_loop(0, send.shape[0], step, 0, unroll=4)


def eliminate(work):
    row = lax.broadcasted_iota(jnp.int32, (LEAF, HALF), 0)
    col = lax.broadcasted_iota(jnp.int32, (LEAF, HALF), 1)

    def spread(value, index):
        return jnp.broadcast_to(value[index : index + 1, :], (LEAF, HALF))

    for base in range(0, HALF, LEAF):
        left = work[base : base + LEAF, :HALF]
        right = work[base : base + LEAF, HALF:]
        wide = [jnp.broadcast_to(left[:, base + c : base + c + 1], (LEAF, HALF)) for c in range(LEAF)]
        pivots = jnp.ones((LEAF, HALF), F32)
        for j in range(0, LEAF, 2):
            c0, c1 = wide[j], wide[j + 1]
            a, b, c = spread(c0, j), spread(c0, j + 1), spread(c1, j + 1)
            scale = 1.0 / (a * c - b * b)
            below = row > j + 1
            m0 = jnp.where(below, c0 * c - c1 * b, 0.0) * scale
            m1 = jnp.where(below, c1 * a - c0 * b, 0.0) * scale
            for k in range(j + 2, LEAF):
                wide[k] = wide[k] - (m0 * spread(c0, k) + m1 * spread(c1, k))
            ratio = b / a
            m0 = jnp.where(row == j + 1, ratio, m0)
            pivots = jnp.where(row == j, a, jnp.where(row == j + 1, c - b * ratio, pivots))
            left = left - (m0 * spread(left, j) + m1 * spread(left, j + 1))
            right = right - (m0 * spread(right, j) + m1 * spread(right, j + 1))
        unit = lax.rsqrt(pivots)
        unit = unit * (1.5 - 0.5 * pivots * unit * unit)
        upper = jnp.where(col >= row + base, left * unit, 0.0)
        right = right * unit
        work[base : base + LEAF, :HALF] = upper
        work[base : base + LEAF, HALF:] = right
        if base + LEAF < HALF:
            beyond = upper.T[base + LEAF :]
            both = jnp.concatenate([upper, right], axis=1)
            product = exact_dot(beyond, both, 1, 0)
            work[base + LEAF :, :] = work[base + LEAF :, :] - product


def exact_dot(left, right, left_dim, right_dim):
    return lax.dot_general(
        left,
        right,
        (((left_dim,), (right_dim,)), ((), ())),
        preferred_element_type=F32,
        precision=lax.Precision.HIGHEST,
    )


def pivot(block, work):
    square = lax.broadcasted_iota(jnp.int32, (HALF, HALF), 0) == lax.broadcasted_iota(jnp.int32, (HALF, HALF), 1)
    eye = jnp.where(square, 1.0, 0.0)
    zero = jnp.zeros((HALF, HALF), F32)
    work[:, :HALF] = block[:HALF, :HALF]
    work[:, HALF:] = eye
    eliminate(work)
    g11 = work[:, :HALF].T
    h11 = work[:, HALF:]
    g21 = exact_dot(block[HALF:, :HALF], h11, 1, 1)
    work[:, :HALF] = block[HALF:, HALF:] - exact_dot(g21, g21, 1, 1)
    work[:, HALF:] = eye
    eliminate(work)
    g22 = work[:, :HALF].T
    h22 = work[:, HALF:]
    h21 = -exact_dot(h22, exact_dot(g21, h11, 1, 0), 1, 0)
    lower = jnp.concatenate([jnp.concatenate([g11, zero], 1), jnp.concatenate([g21, g22], 1)], 0)
    inverse = jnp.concatenate([jnp.concatenate([h11, zero], 1), jnp.concatenate([h21, h22], 1)], 0)
    return lower, inverse


def panel_steps(matrix, top, inverse, work):
    row = lax.broadcasted_iota(jnp.int32, (TOP, PW), 0)

    def step(index, carry):
        a = pl.multiple_of(index * PW, PW)
        here = pl.ds(a, PW)
        lower, inner = pivot(matrix[here, here], work)
        parts = split3(inner)
        for number in range(3):
            inverse[index, number] = parts[number]
        below = matrix[:, here].astype(BF16)
        solved = dot_nt(below, parts[0]) + (dot_nt(below, parts[1]) + dot_nt(below, parts[2]))
        solved = jnp.where(row >= a + PW, solved, 0.0).astype(BF16)
        top[:, here] = solved
        top[here, here] = lower.astype(BF16)
        for part in range(PANELS):
            cols = slice(part * PW, (part + 1) * PW)
            matrix[:, cols] = rounded(matrix[:, cols] - dot_nt(solved, solved[cols]))
        return carry

    lax.fori_loop(0, PANELS, step, 0)


def front_kernel(table, place, gathered, received, diag, top_diag, out, panels, factor, matrix, top, inverse, work, sems):
    device, active = place[0], place[1]
    blocks = CHUNK // BLK
    count = TOP // BLK
    early = pltpu.make_async_copy(gathered.at[:count], panels.at[:count], sems.at[0])
    late = pltpu.make_async_copy(gathered.at[count:], panels.at[count:], sems.at[1])
    early.start()
    late.start()

    def row_block(block):
        total = None
        for slot in range(2):
            source = table[slot * 128 + block]
            part = panels[jnp.maximum(source, 0), slot * BLK : (slot + 1) * BLK, :].astype(F32)
            part = jnp.where(source >= 0, part, 0.0)
            total = part if total is None else total + part
        return total

    early.wait()
    for block in range(count):
        on = lax.broadcasted_iota(jnp.int32, (BLK, TOP), 0) + block * BLK == lax.broadcasted_iota(
            jnp.int32, (BLK, TOP), 1
        )
        total = row_block(block) + jnp.where(on, top_diag[...], 0.0)
        matrix[block * BLK : (block + 1) * BLK, :] = rounded(total)
    panel_steps(matrix, top, inverse, work)
    late.wait()

    def solve(chunk, carry):
        first = chunk * blocks
        for block in range(blocks):
            spot = pl.ds(pl.multiple_of((first + block) * BLK, BLK), BLK)
            factor[spot, :] = row_block(first + block).astype(BF16)
        spot = pl.ds(pl.multiple_of(chunk * CHUNK, CHUNK), CHUNK)
        for step in range(PANELS):
            a, e = step * PW, (step + 1) * PW
            panel = factor[spot, a:e]
            for before in range(step):
                b0, b1 = before * PW, (before + 1) * PW
                panel = (panel.astype(F32) - dot_nt(factor[spot, b0:b1], top[a:e, b0:b1])).astype(BF16)
            solved = dot_nt(panel, inverse[step, 0]) + (dot_nt(panel, inverse[step, 1]) + dot_nt(panel, inverse[step, 2]))
            factor[spot, a:e] = solved.astype(BF16)
        return carry

    lax.fori_loop(0, factor.shape[0] // CHUNK, solve, 0)
    factor[:TOP, :] = top[...]
    own = factor[pl.ds(pl.multiple_of(device * ROWS, ROWS), ROWS), :]
    cols = device * ROWS + lax.broadcasted_iota(jnp.int32, (BLK, ROWS), 1)

    def update(chunk, carry):
        first = chunk * blocks
        tiles = []
        for block in range(blocks):
            total = jnp.zeros((BLK, ROWS), F32)
            for slot in range(2):
                source = table[slot * 128 + first + block]
                part = received[jnp.maximum(source, 0), slot * BLK : (slot + 1) * BLK, :].astype(F32)
                total = total + jnp.where(source >= 0, part, 0.0)
            rows = (first + block) * BLK + lax.broadcasted_iota(jnp.int32, (BLK, ROWS), 0)
            on = rows == cols
            total = total + jnp.where(on, diag[...], 0.0)
            outside = (rows >= active) | (cols >= active)
            tiles.append(jnp.where(outside, jnp.where(on, 1.0, 0.0), total))
        tile = rounded(jnp.concatenate(tiles, axis=0))
        spot = pl.ds(pl.multiple_of(chunk * CHUNK, CHUNK), CHUNK)
        for step in range(PANELS):
            a, e = step * PW, (step + 1) * PW
            tile = rounded(tile - dot_nt(factor[spot, a:e], own[:, a:e]))
        tile = jnp.where(device < TOP // ROWS, 0.0, tile)
        out[:, spot] = tile.T.astype(BF16)
        return carry

    lax.fori_loop(0, factor.shape[0] // CHUNK, update, 0)
    out[:, :TOP] = own


def body(front_diag, children, parent, front_blocks, child_blocks, row_map):
    leaf = lax.axis_index("leaf")
    grid = lax.axis_index("grid")
    devices = lax.axis_size("grid")
    front_order = front_diag.shape[1] * devices
    smem = pl.BlockSpec(memory_space=pltpu.SMEM)
    vmem = pl.BlockSpec(memory_space=pltpu.VMEM)
    anywhere = pl.BlockSpec(memory_space=pl.ANY)
    params = pltpu.CompilerParams(vmem_limit_bytes=VMEM_LIMIT)

    narrow = children[:, :, :TOP]
    panel = pl.pallas_call(
        panel_kernel,
        out_shape=jax.ShapeDtypeStruct((2 * BLK, TOP), BF16),
        in_specs=[smem, smem, smem, smem, vmem, vmem],
        out_specs=vmem,
        compiler_params=params,
    )(leaf.astype(jnp.int32).reshape(1), parent, child_blocks, row_map.reshape(-1), narrow, swapped(narrow))
    gathered = lax.all_gather(panel, "grid", axis=0, tiled=False)

    children, parent, panel = lax.optimization_barrier((children, parent, panel))
    first_own = 2 * leaf
    first_far = 2 * jnp.bitwise_xor(leaf, 1)
    own_slot = jnp.where(parent[first_own] == leaf, 0, 1).astype(jnp.int32)
    far_slot = jnp.where(parent[first_far] == leaf, 0, 1).astype(jnp.int32)
    arrived = swapped(lax.dynamic_index_in_dim(children, 1 - own_slot, 0, keepdims=False))
    ids = jnp.stack([first_own + own_slot, first_far + far_slot])
    maps = row_map[ids]
    numbers = jnp.arange(maps.shape[1], dtype=jnp.int32)
    live = numbers[None, :] < child_blocks[ids][:, None]
    hit = (maps[:, :, None] == jnp.arange(front_order // BLK)[None, None, :]) & live[:, :, None]
    table = jnp.max(jnp.where(hit, numbers[None, :, None], -1), axis=1).reshape(-1)
    send = pl.pallas_call(
        pack_kernel,
        out_shape=jax.ShapeDtypeStruct((devices, SENT, 128), BF16),
        in_specs=[smem, smem, vmem, vmem, vmem],
        out_specs=vmem,
        compiler_params=params,
    )(table, own_slot.reshape(1), children, arrived, front_diag)
    received = lax.all_to_all(send, "grid", 0, 0, tiled=True)
    parts = received[: TOP // ROWS, 2 * BLK : 2 * BLK + 3, :].astype(F32)
    top_diag = (parts[:, 0] + parts[:, 1] + parts[:, 2]).reshape(1, TOP)
    place = jnp.stack([grid, front_blocks[leaf] * BLK]).astype(jnp.int32)
    factor = pl.pallas_call(
        front_kernel,
        out_shape=jax.ShapeDtypeStruct((ROWS, front_order), BF16),
        in_specs=[smem, smem, anywhere, vmem, vmem, vmem],
        out_specs=vmem,
        scratch_shapes=[
            pltpu.VMEM((devices, 2 * BLK, TOP), BF16),
            pltpu.VMEM((front_order, TOP), BF16),
            pltpu.VMEM((TOP, TOP), F32),
            pltpu.VMEM((TOP, TOP), BF16),
            pltpu.VMEM((PANELS, 3, PW, PW), BF16),
            pltpu.VMEM((HALF, 2 * HALF), F32),
            pltpu.SemaphoreType.DMA((2,)),
        ],
        compiler_params=params,
    )(table, place, gathered, received, front_diag, top_diag)
    return factor[None]


def solution(mesh):
    in_specs = (P("leaf", "grid"), P("leaf", "grid", None), P(), P(), P(), P())
    return jax.shard_map(body, mesh=mesh, in_specs=in_specs, out_specs=P("leaf", "grid", None), check_vma=False)
```

```python
import jax
import jax.numpy as jnp
from jax import lax
from jax.experimental import pallas as pl
from jax.experimental.pallas import tpu as pltpu
from jax.sharding import PartitionSpec as P

BLK = 64
PW = 256
PANELS = 3
TOP = PW * PANELS
ROWS = 128
SENT = 144
LEAF = 16
HALF = 128
CHUNK = 1024
F32 = jnp.float32
BF16 = jnp.bfloat16
VMEM_LIMIT = 56 * 1024 * 1024


def swapped(value):
    pairs = [(source, source ^ 1) for source in range(lax.axis_size("leaf"))]
    return lax.ppermute(value, "leaf", pairs)


def split3(value):
    high = value.astype(BF16)
    rest = value - high.astype(F32)
    middle = rest.astype(BF16)
    low = (rest - middle.astype(F32)).astype(BF16)
    return high, middle, low


def dot_nt(left, right):
    return lax.dot_general(left, right, (((1,), (1,)), ((), ())), preferred_element_type=F32)


def rounded(value):
    return value.astype(BF16).astype(F32)


def spread_tile(child, first, second):
    lanes = lax.broadcasted_iota(jnp.int32, (BLK, 2 * BLK), 1)

    def half(block, side):
        index = jnp.maximum(block, 0)
        tile = child(pl.ds(pl.multiple_of((index // 2) * 128, 128), 128)).astype(F32)
        tile = jnp.where(index % 2 == side, tile, pltpu.roll(tile, BLK, 1))
        return jnp.where(block >= 0, tile, 0.0)

    return jnp.where(lanes < BLK, half(first, 0), half(second, 1)).astype(BF16)


def panel_kernel(leaf, parent, counts, row_map, children, arrived, panel):
    own_slot = jnp.where(parent[2 * leaf[0]] == leaf[0], 0, 1)
    far_first = 2 * jnp.bitwise_xor(leaf[0], 1)
    far_slot = jnp.where(parent[far_first] == leaf[0], 0, 1)
    for slot, source, pick, child_id in (
        (0, children, own_slot, 2 * leaf[0] + own_slot),
        (1, arrived, far_slot, far_first + far_slot),
    ):
        places = [
            jnp.where(block < counts[child_id], row_map[child_id * 64 + block], -1) for block in range(TOP // BLK)
        ]

        def find(target):
            found = jnp.int32(-1)
            for block, place in enumerate(places):
                found = jnp.where(place == target, block, found)
            return found

        def child(cols):
            return source[pick, :, cols]

        for pair in range(TOP // 128):
            tile = spread_tile(child, find(2 * pair), find(2 * pair + 1))
            panel[slot * BLK : (slot + 1) * BLK, pair * 128 : (pair + 1) * 128] = tile


def pack_kernel(table, pick, children, arrived, diag, send):
    def own(cols):
        return children[pick[0], :, cols]

    def far(cols):
        return arrived[:, cols]

    parts = split3(diag[...])
    tail = jnp.concatenate([part.astype(F32) for part in parts] + [jnp.zeros((13, 128), F32)], axis=0).astype(BF16)

    def step(pair, carry):
        for slot, child in ((0, own), (1, far)):
            send[pair, slot * BLK : (slot + 1) * BLK, :] = spread_tile(
                child, table[slot * 128 + 2 * pair], table[slot * 128 + 2 * pair + 1]
            )
        send[pair, 2 * BLK : SENT, :] = tail
        return carry

    lax.fori_loop(0, send.shape[0], step, 0, unroll=4)


def eliminate(work, fill):
    row = lax.broadcasted_iota(jnp.int32, (LEAF, HALF), 0)
    col = lax.broadcasted_iota(jnp.int32, (LEAF, HALF), 1)

    def spread(value, index):
        return jnp.broadcast_to(value[index : index + 1, :], (LEAF, HALF))

    for base in range(0, HALF, LEAF):
        fill()
        left = work[base : base + LEAF, :HALF]
        right = work[base : base + LEAF, HALF:]
        wide = [jnp.broadcast_to(left[:, base + c : base + c + 1], (LEAF, HALF)) for c in range(LEAF)]
        pivots = jnp.ones((LEAF, HALF), F32)
        for j in range(0, LEAF, 2):
            c0, c1 = wide[j], wide[j + 1]
            a, b, c = spread(c0, j), spread(c0, j + 1), spread(c1, j + 1)
            scale = 1.0 / (a * c - b * b)
            below = row > j + 1
            m0 = jnp.where(below, c0 * c - c1 * b, 0.0) * scale
            m1 = jnp.where(below, c1 * a - c0 * b, 0.0) * scale
            for k in range(j + 2, LEAF):
                wide[k] = wide[k] - (m0 * spread(c0, k) + m1 * spread(c1, k))
            ratio = b / a
            m0 = jnp.where(row == j + 1, ratio, m0)
            pivots = jnp.where(row == j, a, jnp.where(row == j + 1, c - b * ratio, pivots))
            left = left - (m0 * spread(left, j) + m1 * spread(left, j + 1))
            right = right - (m0 * spread(right, j) + m1 * spread(right, j + 1))
        unit = lax.rsqrt(pivots)
        unit = unit * (1.5 - 0.5 * pivots * unit * unit)
        upper = jnp.where(col >= row + base, left * unit, 0.0)
        right = right * unit
        work[base : base + LEAF, :HALF] = upper
        work[base : base + LEAF, HALF:] = right
        if base + LEAF < HALF:
            beyond = upper.T[base + LEAF :]
            both = jnp.concatenate([upper, right], axis=1)
            product = exact_dot(beyond, both, 1, 0)
            work[base + LEAF :, :] = work[base + LEAF :, :] - product


def exact_dot(left, right, left_dim, right_dim):
    return lax.dot_general(
        left,
        right,
        (((left_dim,), (right_dim,)), ((), ())),
        preferred_element_type=F32,
        precision=lax.Precision.HIGHEST,
    )


def pivot(block, work, fill):
    square = lax.broadcasted_iota(jnp.int32, (HALF, HALF), 0) == lax.broadcasted_iota(jnp.int32, (HALF, HALF), 1)
    eye = jnp.where(square, 1.0, 0.0)
    zero = jnp.zeros((HALF, HALF), F32)
    work[:, :HALF] = block[:HALF, :HALF]
    work[:, HALF:] = eye
    eliminate(work, fill)
    g11 = work[:, :HALF].T
    h11 = work[:, HALF:]
    g21 = exact_dot(block[HALF:, :HALF], h11, 1, 1)
    work[:, :HALF] = block[HALF:, HALF:] - exact_dot(g21, g21, 1, 1)
    work[:, HALF:] = eye
    eliminate(work, fill)
    g22 = work[:, :HALF].T
    h22 = work[:, HALF:]
    h21 = -exact_dot(h22, exact_dot(g21, h11, 1, 0), 1, 0)
    lower = jnp.concatenate([jnp.concatenate([g11, zero], 1), jnp.concatenate([g21, g22], 1)], 0)
    inverse = jnp.concatenate([jnp.concatenate([h11, zero], 1), jnp.concatenate([h21, h22], 1)], 0)
    return lower, inverse


def assemble_kernel(table, place, received, diag, base):
    device, active = place[0], place[1]
    cols = device * ROWS + lax.broadcasted_iota(jnp.int32, (BLK, ROWS), 1)

    def step(block, carry):
        total = None
        for slot in range(2):
            source = table[slot * 128 + block]
            part = received[jnp.maximum(source, 0), slot * BLK : (slot + 1) * BLK, :].astype(F32)
            part = jnp.where(source >= 0, part, 0.0)
            total = part if total is None else total + part
        rows = block * BLK + lax.broadcasted_iota(jnp.int32, (BLK, ROWS), 0)
        on = rows == cols
        total = total + jnp.where(on, diag[...], 0.0)
        outside = (rows >= active) | (cols >= active)
        total = jnp.where(outside, jnp.where(on, 1.0, 0.0), total)
        base[pl.ds(pl.multiple_of(block * BLK, BLK), BLK), :] = total.astype(BF16)
        return carry

    lax.fori_loop(0, base.shape[0] // BLK, step, 0, unroll=4)


def front_kernel(table, place, gathered, base, top_diag, out, panels, factor, trail, matrix, top, inverse, work, sems):
    device = place[0]
    start = pl.multiple_of(device * ROWS, ROWS)
    count = TOP // BLK
    jobs = 2 * (HALF // LEAF)
    rows = factor.shape[0] // jobs
    early = pltpu.make_async_copy(gathered.at[:count], panels.at[:count], sems.at[0])
    late = pltpu.make_async_copy(gathered.at[count:], panels.at[count:], sems.at[1])
    early.start()
    late.start()

    def row_block(block):
        total = None
        for slot in range(2):
            source = table[slot * 128 + block]
            part = panels[jnp.maximum(source, 0), slot * BLK : (slot + 1) * BLK, :].astype(F32)
            part = jnp.where(source >= 0, part, 0.0)
            total = part if total is None else total + part
        return total

    def gather_rows(job):
        if job == 0:
            late.wait()
        for block in range(job * rows // BLK, (job + 1) * rows // BLK):
            factor[block * BLK : (block + 1) * BLK, :] = row_block(block).astype(BF16)

    def solved_rows(panel, step):
        return (dot_nt(panel, inverse[step, 0]) + (dot_nt(panel, inverse[step, 1]) + dot_nt(panel, inverse[step, 2]))).astype(BF16)

    def solve_rows(step, job):
        spot = slice(job * rows, (job + 1) * rows)
        a, e = step * PW, (step + 1) * PW
        solved = solved_rows(factor[spot, a:e], step)
        factor[spot, a:e] = solved
        for after in range(step + 1, PANELS):
            b0, b1 = after * PW, (after + 1) * PW
            factor[spot, b0:b1] = (factor[spot, b0:b1].astype(F32) - dot_nt(solved, top[b0:b1, a:e])).astype(BF16)

    def update_rows(job):
        spot = slice(job * rows, (job + 1) * rows)
        own = factor[pl.ds(start, ROWS), :PW]
        trail[spot, :] = (base[spot, :].astype(F32) - dot_nt(factor[spot, :PW], own)).astype(BF16)

    early.wait()
    for block in range(count):
        on = lax.broadcasted_iota(jnp.int32, (BLK, TOP), 0) + block * BLK == lax.broadcasted_iota(
            jnp.int32, (BLK, TOP), 1
        )
        total = row_block(block) + jnp.where(on, top_diag[...], 0.0)
        matrix[block * BLK : (block + 1) * BLK, :] = rounded(total)
    top[...] = jnp.zeros_like(top)
    for step in range(PANELS):
        a, e = step * PW, (step + 1) * PW
        waiting = list(range(jobs))

        def fill(step=step, waiting=waiting):
            job = waiting.pop(0)
            if step == 0:
                gather_rows(job)
            else:
                solve_rows(step - 1, job)
                if step == PANELS - 1:
                    update_rows(job)

        lower, inner = pivot(matrix[a:e, a:e], work, fill)
        parts = split3(inner)
        for number in range(3):
            inverse[step, number] = parts[number]
        top[a:e, a:e] = lower.astype(BF16)
        if e < TOP:
            solved = solved_rows(matrix[e:, a:e].astype(BF16), step)
            top[e:, a:e] = solved
            matrix[e:, e:] = rounded(matrix[e:, e:] - dot_nt(solved, solved))

    last = TOP - PW
    mine = jnp.concatenate(
        [factor[pl.ds(start, ROWS), :last], solved_rows(factor[pl.ds(start, ROWS), last:], PANELS - 1)], axis=1
    )
    leading = device < TOP // ROWS
    own = jnp.where(leading, top[pl.ds(pl.multiple_of(jnp.minimum(start, TOP - ROWS), ROWS), ROWS), :], mine)

    def update(chunk, carry):
        spot = pl.ds(pl.multiple_of(chunk * CHUNK, CHUNK), CHUNK)
        tile = trail[spot, :].astype(F32)
        for step in range(1, PANELS):
            a, e = step * PW, (step + 1) * PW
            part = factor[spot, a:e]
            if e == TOP:
                part = solved_rows(part, step)
            tile = rounded(tile - dot_nt(part, own[:, a:e]))
        tile = jnp.where(leading, 0.0, tile)
        out[:, spot] = tile.T.astype(BF16)
        return carry

    lax.fori_loop(0, factor.shape[0] // CHUNK, update, 0)
    out[:, :TOP] = own


def body(front_diag, children, parent, front_blocks, child_blocks, row_map):
    leaf = lax.axis_index("leaf")
    grid = lax.axis_index("grid")
    devices = lax.axis_size("grid")
    front_order = front_diag.shape[1] * devices
    smem = pl.BlockSpec(memory_space=pltpu.SMEM)
    vmem = pl.BlockSpec(memory_space=pltpu.VMEM)
    anywhere = pl.BlockSpec(memory_space=pl.ANY)
    params = pltpu.CompilerParams(vmem_limit_bytes=VMEM_LIMIT)

    narrow = children[:, :, :TOP]
    panel = pl.pallas_call(
        panel_kernel,
        out_shape=jax.ShapeDtypeStruct((2 * BLK, TOP), BF16),
        in_specs=[smem, smem, smem, smem, vmem, vmem],
        out_specs=vmem,
        compiler_params=params,
    )(leaf.astype(jnp.int32).reshape(1), parent, child_blocks, row_map.reshape(-1), narrow, swapped(narrow))
    gathered = lax.all_gather(panel, "grid", axis=0, tiled=False)

    children, parent, panel = lax.optimization_barrier((children, parent, panel))
    first_own = 2 * leaf
    first_far = 2 * jnp.bitwise_xor(leaf, 1)
    own_slot = jnp.where(parent[first_own] == leaf, 0, 1).astype(jnp.int32)
    far_slot = jnp.where(parent[first_far] == leaf, 0, 1).astype(jnp.int32)
    arrived = swapped(lax.dynamic_index_in_dim(children, 1 - own_slot, 0, keepdims=False))
    ids = jnp.stack([first_own + own_slot, first_far + far_slot])
    maps = row_map[ids]
    numbers = jnp.arange(maps.shape[1], dtype=jnp.int32)
    live = numbers[None, :] < child_blocks[ids][:, None]
    hit = (maps[:, :, None] == jnp.arange(front_order // BLK)[None, None, :]) & live[:, :, None]
    table = jnp.max(jnp.where(hit, numbers[None, :, None], -1), axis=1).reshape(-1)
    send = pl.pallas_call(
        pack_kernel,
        out_shape=jax.ShapeDtypeStruct((devices, SENT, 128), BF16),
        in_specs=[smem, smem, vmem, vmem, vmem],
        out_specs=vmem,
        compiler_params=params,
    )(table, own_slot.reshape(1), children, arrived, front_diag)
    received = lax.all_to_all(send, "grid", 0, 0, tiled=True)
    parts = received[: TOP // ROWS, 2 * BLK : 2 * BLK + 3, :].astype(F32)
    top_diag = (parts[:, 0] + parts[:, 1] + parts[:, 2]).reshape(1, TOP)
    place = jnp.stack([grid, front_blocks[leaf] * BLK]).astype(jnp.int32)
    base = pl.pallas_call(
        assemble_kernel,
        out_shape=jax.ShapeDtypeStruct((front_order, ROWS), BF16),
        in_specs=[smem, smem, vmem, vmem],
        out_specs=vmem,
        compiler_params=params,
    )(table, place, received, front_diag)
    factor = pl.pallas_call(
        front_kernel,
        out_shape=jax.ShapeDtypeStruct((ROWS, front_order), BF16),
        in_specs=[smem, smem, anywhere, vmem, vmem],
        out_specs=vmem,
        scratch_shapes=[
            pltpu.VMEM((devices, 2 * BLK, TOP), BF16),
            pltpu.VMEM((front_order, TOP), BF16),
            pltpu.VMEM((front_order, ROWS), BF16),
            pltpu.VMEM((TOP, TOP), F32),
            pltpu.VMEM((TOP, TOP), BF16),
            pltpu.VMEM((PANELS, 3, PW, PW), BF16),
            pltpu.VMEM((HALF, 2 * HALF), F32),
            pltpu.SemaphoreType.DMA((2,)),
        ],
        compiler_params=params,
    )(table, place, gathered, base, top_diag)
    return factor[None]


def solution(mesh):
    in_specs = (P("leaf", "grid"), P("leaf", "grid", None), P(), P(), P(), P())
    return jax.shard_map(body, mesh=mesh, in_specs=in_specs, out_specs=P("leaf", "grid", None), check_vma=False)
```

```python
import jax
import jax.numpy as jnp
from jax import lax
from jax.experimental import pallas as pl
from jax.experimental.pallas import tpu as pltpu
from jax.sharding import PartitionSpec as P

BLK = 64
PW = 256
PANELS = 3
TOP = PW * PANELS
ROWS = 128
SENT = 128
LEAF = 16
HALF = 128
CHUNK = 1024
F32 = jnp.float32
BF16 = jnp.bfloat16
VMEM_LIMIT = 56 * 1024 * 1024


def swapped(value):
    pairs = [(source, source ^ 1) for source in range(lax.axis_size("leaf"))]
    return lax.ppermute(value, "leaf", pairs)


def split3(value):
    high = value.astype(BF16)
    rest = value - high.astype(F32)
    middle = rest.astype(BF16)
    low = (rest - middle.astype(F32)).astype(BF16)
    return high, middle, low


def dot_nt(left, right):
    return lax.dot_general(left, right, (((1,), (1,)), ((), ())), preferred_element_type=F32)


def rounded(value):
    return value.astype(BF16).astype(F32)


def spread_tile(child, first, second):
    lanes = lax.broadcasted_iota(jnp.int32, (BLK, 2 * BLK), 1)

    def half(block, side):
        index = jnp.maximum(block, 0)
        tile = child(pl.ds(pl.multiple_of((index // 2) * 128, 128), 128)).astype(F32)
        tile = jnp.where(index % 2 == side, tile, pltpu.roll(tile, BLK, 1))
        return jnp.where(block >= 0, tile, 0.0)

    return jnp.where(lanes < BLK, half(first, 0), half(second, 1)).astype(BF16)


def panel_kernel(leaf, parent, counts, row_map, children, arrived, panel):
    own_slot = jnp.where(parent[2 * leaf[0]] == leaf[0], 0, 1)
    far_first = 2 * jnp.bitwise_xor(leaf[0], 1)
    far_slot = jnp.where(parent[far_first] == leaf[0], 0, 1)
    for slot, source, pick, child_id in (
        (0, children, own_slot, 2 * leaf[0] + own_slot),
        (1, arrived, far_slot, far_first + far_slot),
    ):
        places = [
            jnp.where(block < counts[child_id], row_map[child_id, block], -1) for block in range(TOP // BLK)
        ]

        def find(target):
            found = jnp.int32(-1)
            for block, place in enumerate(places):
                found = jnp.where(place == target, block, found)
            return found

        def child(cols):
            return source[pick, :, cols]

        for pair in range(TOP // 128):
            tile = spread_tile(child, find(2 * pair), find(2 * pair + 1))
            panel[slot * BLK : (slot + 1) * BLK, pair * 128 : (pair + 1) * 128] = tile


def pack_kernel(table, pick, children, arrived, send):
    def own(cols):
        return children[pick[0], :, cols]

    def far(cols):
        return arrived[:, cols]

    def step(pair, carry):
        for slot, child in ((0, own), (1, far)):
            send[pair, slot * BLK : (slot + 1) * BLK, :] = spread_tile(
                child, table[slot * 128 + 2 * pair], table[slot * 128 + 2 * pair + 1]
            )
        return carry

    lax.fori_loop(0, send.shape[0], step, 0, unroll=4)


def eliminate(work, fill):
    row = lax.broadcasted_iota(jnp.int32, (LEAF, HALF), 0)
    col = lax.broadcasted_iota(jnp.int32, (LEAF, HALF), 1)

    def spread(value, index):
        return jnp.broadcast_to(value[index : index + 1, :], (LEAF, HALF))

    def columns(value, base):
        return [jnp.broadcast_to(value[:, base + c : base + c + 1], (LEAF, HALF)) for c in range(LEAF)]

    left = work[:LEAF, :HALF]
    right = work[:LEAF, HALF:]
    wide = columns(left, 0)
    for base in range(0, HALF, LEAF):
        fill()
        more = base + LEAF < HALF
        if more:
            next_left = work[base + LEAF : base + 2 * LEAF, :HALF]
            next_right = work[base + LEAF : base + 2 * LEAF, HALF:]
            cross = columns(next_left, base)
        pivots = jnp.ones((LEAF, HALF), F32)
        for j in range(0, LEAF, 2):
            c0, c1 = wide[j], wide[j + 1]
            a, b, c = spread(c0, j), spread(c0, j + 1), spread(c1, j + 1)
            scale = 1.0 / (a * c - b * b)
            below = row > j + 1
            m0 = jnp.where(below, c0 * c - c1 * b, 0.0) * scale
            m1 = jnp.where(below, c1 * a - c0 * b, 0.0) * scale
            l0, l1 = spread(left, j), spread(left, j + 1)
            r0, r1 = spread(right, j), spread(right, j + 1)
            for k in range(j + 2, LEAF):
                wide[k] = wide[k] - (m0 * spread(c0, k) + m1 * spread(c1, k))
            if more:
                d0, d1 = cross[j], cross[j + 1]
                n0 = (d0 * c - d1 * b) * scale
                n1 = (d1 * a - d0 * b) * scale
                for k in range(j + 2, LEAF):
                    cross[k] = cross[k] - (n0 * spread(c0, k) + n1 * spread(c1, k))
                next_left = next_left - (n0 * l0 + n1 * l1)
                next_right = next_right - (n0 * r0 + n1 * r1)
            ratio = b / a
            m0 = jnp.where(row == j + 1, ratio, m0)
            pivots = jnp.where(row == j, a, jnp.where(row == j + 1, c - b * ratio, pivots))
            left = left - (m0 * l0 + m1 * l1)
            right = right - (m0 * r0 + m1 * r1)
        unit = lax.rsqrt(pivots)
        unit = unit * (1.5 - 0.5 * pivots * unit * unit)
        upper = jnp.where(col >= row + base, left * unit, 0.0)
        right = right * unit
        work[base : base + LEAF, :HALF] = upper
        work[base : base + LEAF, HALF:] = right
        if base + 2 * LEAF < HALF:
            beyond = upper.T[base + 2 * LEAF :]
            both = jnp.concatenate([upper, right], axis=1)
            product = exact_dot(beyond, both, 1, 0)
            work[base + 2 * LEAF :, :] = work[base + 2 * LEAF :, :] - product
        if more:
            left, right = next_left, next_right
            wide = columns(left, base + LEAF)


def exact_dot(left, right, left_dim, right_dim):
    return lax.dot_general(
        left,
        right,
        (((left_dim,), (right_dim,)), ((), ())),
        preferred_element_type=F32,
        precision=lax.Precision.HIGHEST,
    )


def pivot(block, work, fill):
    square = lax.broadcasted_iota(jnp.int32, (HALF, HALF), 0) == lax.broadcasted_iota(jnp.int32, (HALF, HALF), 1)
    eye = jnp.where(square, 1.0, 0.0)
    zero = jnp.zeros((HALF, HALF), F32)
    work[:, :HALF] = block[:HALF, :HALF]
    work[:, HALF:] = eye
    eliminate(work, fill)
    g11 = work[:, :HALF].T
    h11 = work[:, HALF:]
    g21 = exact_dot(block[HALF:, :HALF], h11, 1, 1)
    work[:, :HALF] = block[HALF:, HALF:] - exact_dot(g21, g21, 1, 1)
    work[:, HALF:] = eye
    eliminate(work, fill)
    g22 = work[:, :HALF].T
    h22 = work[:, HALF:]
    h21 = -exact_dot(h22, exact_dot(g21, h11, 1, 0), 1, 0)
    lower = jnp.concatenate([jnp.concatenate([g11, zero], 1), jnp.concatenate([g21, g22], 1)], 0)
    inverse = jnp.concatenate([jnp.concatenate([h11, zero], 1), jnp.concatenate([h21, h22], 1)], 0)
    return lower, inverse


def assemble_kernel(table, place, received, diag, base):
    device, active = place[0], place[1]
    cols = device * ROWS + lax.broadcasted_iota(jnp.int32, (BLK, ROWS), 1)

    def step(block, carry):
        total = None
        for slot in range(2):
            source = table[slot * 128 + block]
            part = received[jnp.maximum(source, 0), slot * BLK : (slot + 1) * BLK, :].astype(F32)
            part = jnp.where(source >= 0, part, 0.0)
            total = part if total is None else total + part
        rows = block * BLK + lax.broadcasted_iota(jnp.int32, (BLK, ROWS), 0)
        on = rows == cols
        total = total + jnp.where(on, diag[...], 0.0)
        outside = (rows >= active) | (cols >= active)
        total = jnp.where(outside, jnp.where(on, 1.0, 0.0), total)
        base[pl.ds(pl.multiple_of(block * BLK, BLK), BLK), :] = total.astype(BF16)
        return carry

    lax.fori_loop(0, base.shape[0] // BLK, step, 0, unroll=4)


def front_kernel(table, place, gathered, base, top_diag, out, panels, factor, trail, matrix, top, inverse, work, sems):
    device = place[0]
    start = pl.multiple_of(device * ROWS, ROWS)
    count = TOP // BLK
    jobs = 2 * (HALF // LEAF)
    rows = factor.shape[0] // jobs
    early = pltpu.make_async_copy(gathered.at[:count], panels.at[:count], sems.at[0])
    late = pltpu.make_async_copy(gathered.at[count:], panels.at[count:], sems.at[1])
    early.start()
    late.start()

    def row_block(block):
        total = None
        for slot in range(2):
            source = table[slot * 128 + block]
            part = panels[jnp.maximum(source, 0), slot * BLK : (slot + 1) * BLK, :].astype(F32)
            part = jnp.where(source >= 0, part, 0.0)
            total = part if total is None else total + part
        return total

    def gather_rows(job):
        if job == 0:
            late.wait()
        for block in range(job * rows // BLK, (job + 1) * rows // BLK):
            factor[block * BLK : (block + 1) * BLK, :] = row_block(block).astype(BF16)

    def solved_rows(panel, step):
        return (dot_nt(panel, inverse[step, 0]) + (dot_nt(panel, inverse[step, 1]) + dot_nt(panel, inverse[step, 2]))).astype(BF16)

    def solve_rows(step, job):
        spot = slice(job * rows, (job + 1) * rows)
        a, e = step * PW, (step + 1) * PW
        solved = solved_rows(factor[spot, a:e], step)
        factor[spot, a:e] = solved
        for after in range(step + 1, PANELS):
            b0, b1 = after * PW, (after + 1) * PW
            factor[spot, b0:b1] = (factor[spot, b0:b1].astype(F32) - dot_nt(solved, top[b0:b1, a:e])).astype(BF16)

    def update_rows(job):
        spot = slice(job * rows, (job + 1) * rows)
        own = factor[pl.ds(start, ROWS), :PW]
        trail[spot, :] = (base[spot, :].astype(F32) - dot_nt(factor[spot, :PW], own)).astype(BF16)

    early.wait()
    for block in range(count):
        on = lax.broadcasted_iota(jnp.int32, (BLK, TOP), 0) + block * BLK == lax.broadcasted_iota(
            jnp.int32, (BLK, TOP), 1
        )
        total = row_block(block) + jnp.where(on, top_diag[...], 0.0)
        matrix[block * BLK : (block + 1) * BLK, :] = rounded(total)
    top[...] = jnp.zeros_like(top)
    for step in range(PANELS):
        a, e = step * PW, (step + 1) * PW
        waiting = list(range(jobs))

        def fill(step=step, waiting=waiting):
            job = waiting.pop(0)
            if step == 0:
                gather_rows(job)
            else:
                solve_rows(step - 1, job)
                if step == PANELS - 1:
                    update_rows(job)

        lower, inner = pivot(matrix[a:e, a:e], work, fill)
        parts = split3(inner)
        for number in range(3):
            inverse[step, number] = parts[number]
        top[a:e, a:e] = lower.astype(BF16)
        if e < TOP:
            solved = solved_rows(matrix[e:, a:e].astype(BF16), step)
            top[e:, a:e] = solved
            matrix[e:, e:] = rounded(matrix[e:, e:] - dot_nt(solved, solved))

    last = TOP - PW
    mine = jnp.concatenate(
        [factor[pl.ds(start, ROWS), :last], solved_rows(factor[pl.ds(start, ROWS), last:], PANELS - 1)], axis=1
    )
    leading = device < TOP // ROWS
    own = jnp.where(leading, top[pl.ds(pl.multiple_of(jnp.minimum(start, TOP - ROWS), ROWS), ROWS), :], mine)

    def update(chunk, carry):
        spot = pl.ds(pl.multiple_of(chunk * CHUNK, CHUNK), CHUNK)
        tile = trail[spot, :].astype(F32)
        for step in range(1, PANELS):
            a, e = step * PW, (step + 1) * PW
            part = factor[spot, a:e]
            if e == TOP:
                part = solved_rows(part, step)
            tile = rounded(tile - dot_nt(part, own[:, a:e]))
        tile = jnp.where(leading, 0.0, tile)
        out[:, spot] = tile.T.astype(BF16)
        return carry

    lax.fori_loop(0, factor.shape[0] // CHUNK, update, 0)
    out[:, :TOP] = own


def body(front_diag, children, parent, front_blocks, child_blocks, row_map):
    leaf = lax.axis_index("leaf")
    grid = lax.axis_index("grid")
    devices = lax.axis_size("grid")
    front_order = front_diag.shape[1] * devices
    smem = pl.BlockSpec(memory_space=pltpu.SMEM)
    vmem = pl.BlockSpec(memory_space=pltpu.VMEM)
    anywhere = pl.BlockSpec(memory_space=pl.ANY)
    params = pltpu.CompilerParams(vmem_limit_bytes=VMEM_LIMIT)

    narrow = children[:, :, :TOP]
    panel = pl.pallas_call(
        panel_kernel,
        out_shape=jax.ShapeDtypeStruct((2 * BLK, TOP), BF16),
        in_specs=[smem, smem, smem, smem, vmem, vmem],
        out_specs=vmem,
        compiler_params=params,
    )(leaf.astype(jnp.int32).reshape(1), parent, child_blocks, row_map, narrow, swapped(narrow))
    gathered = lax.all_gather(panel, "grid", axis=0, tiled=False)

    children, parent, panel = lax.optimization_barrier((children, parent, panel))
    first_own = 2 * leaf
    first_far = 2 * jnp.bitwise_xor(leaf, 1)
    own_slot = jnp.where(parent[first_own] == leaf, 0, 1).astype(jnp.int32)
    far_slot = jnp.where(parent[first_far] == leaf, 0, 1).astype(jnp.int32)
    arrived = swapped(lax.dynamic_index_in_dim(children, 1 - own_slot, 0, keepdims=False))
    ids = jnp.stack([first_own + own_slot, first_far + far_slot])
    maps = row_map[ids]
    numbers = jnp.arange(maps.shape[1], dtype=jnp.int32)
    live = numbers[None, :] < child_blocks[ids][:, None]
    hit = (maps[:, :, None] == jnp.arange(front_order // BLK)[None, None, :]) & live[:, :, None]
    table = jnp.max(jnp.where(hit, numbers[None, :, None], -1), axis=1).reshape(-1)
    send = pl.pallas_call(
        pack_kernel,
        out_shape=jax.ShapeDtypeStruct((devices, SENT, 128), BF16),
        in_specs=[smem, smem, vmem, vmem],
        out_specs=vmem,
        compiler_params=params,
    )(table, own_slot.reshape(1), children, arrived)
    received = lax.all_to_all(send, "grid", 0, 0, tiled=True)
    received, own_diag = lax.optimization_barrier((received, front_diag))
    copies = jnp.broadcast_to(own_diag, (devices, ROWS))
    top_diag = lax.all_to_all(copies, "grid", 0, 0, tiled=True)[: TOP // ROWS].reshape(1, TOP)
    place = jnp.stack([grid, front_blocks[leaf] * BLK]).astype(jnp.int32)
    base = pl.pallas_call(
        assemble_kernel,
        out_shape=jax.ShapeDtypeStruct((front_order, ROWS), BF16),
        in_specs=[smem, smem, vmem, vmem],
        out_specs=vmem,
        compiler_params=params,
    )(table, place, received, front_diag)
    factor = pl.pallas_call(
        front_kernel,
        out_shape=jax.ShapeDtypeStruct((ROWS, front_order), BF16),
        in_specs=[smem, smem, anywhere, vmem, vmem],
        out_specs=vmem,
        scratch_shapes=[
            pltpu.VMEM((devices, 2 * BLK, TOP), BF16),
            pltpu.VMEM((front_order, TOP), BF16),
            pltpu.VMEM((front_order, ROWS), BF16),
            pltpu.VMEM((TOP, TOP), F32),
            pltpu.VMEM((TOP, TOP), BF16),
            pltpu.VMEM((PANELS, 3, PW, PW), BF16),
            pltpu.VMEM((HALF, 2 * HALF), F32),
            pltpu.SemaphoreType.DMA((2,)),
        ],
        compiler_params=params,
    )(table, place, gathered, base, top_diag)
    return factor[None]


def solution(mesh):
    in_specs = (P("leaf", "grid"), P("leaf", "grid", None), P(), P(), P(), P())
    return jax.shard_map(body, mesh=mesh, in_specs=in_specs, out_specs=P("leaf", "grid", None), check_vma=False)
```

```python
import jax
import jax.numpy as jnp
from jax import lax
from jax.experimental import pallas as pl
from jax.experimental.pallas import tpu as pltpu
from jax.sharding import PartitionSpec as P

BLK = 64
PW = 256
PANELS = 3
TOP = PW * PANELS
ROWS = 128
SENT = 128
LEAF = 16
HALF = 128
CHUNK = 1024
F32 = jnp.float32
BF16 = jnp.bfloat16
VMEM_LIMIT = 56 * 1024 * 1024


def swapped(value):
    pairs = [(source, source ^ 1) for source in range(lax.axis_size("leaf"))]
    return lax.ppermute(value, "leaf", pairs)


def split3(value):
    high = value.astype(BF16)
    rest = value - high.astype(F32)
    middle = rest.astype(BF16)
    low = (rest - middle.astype(F32)).astype(BF16)
    return high, middle, low


def dot_nt(left, right):
    return lax.dot_general(left, right, (((1,), (1,)), ((), ())), preferred_element_type=F32)


def rounded(value):
    return value.astype(BF16).astype(F32)


def spread_tile(child, first, second):
    lanes = lax.broadcasted_iota(jnp.int32, (BLK, 2 * BLK), 1)

    def half(block, side):
        index = jnp.maximum(block, 0)
        tile = child(pl.ds(pl.multiple_of((index // 2) * 128, 128), 128)).astype(F32)
        tile = jnp.where(index % 2 == side, tile, pltpu.roll(tile, BLK, 1))
        return jnp.where(block >= 0, tile, 0.0)

    return jnp.where(lanes < BLK, half(first, 0), half(second, 1)).astype(BF16)


def panel_kernel(leaf, parent, counts, row_map, children, arrived, panel):
    own_slot = jnp.where(parent[2 * leaf[0]] == leaf[0], 0, 1)
    far_first = 2 * jnp.bitwise_xor(leaf[0], 1)
    far_slot = jnp.where(parent[far_first] == leaf[0], 0, 1)
    for slot, source, pick, child_id in (
        (0, children, own_slot, 2 * leaf[0] + own_slot),
        (1, arrived, far_slot, far_first + far_slot),
    ):
        places = [
            jnp.where(block < counts[child_id], row_map[child_id, block], -1) for block in range(TOP // BLK)
        ]

        def find(target):
            found = jnp.int32(-1)
            for block, place in enumerate(places):
                found = jnp.where(place == target, block, found)
            return found

        def child(cols):
            return source[pick, :, cols]

        for pair in range(TOP // 128):
            tile = spread_tile(child, find(2 * pair), find(2 * pair + 1))
            panel[slot * BLK : (slot + 1) * BLK, pair * 128 : (pair + 1) * 128] = tile


def pack_kernel(table, pick, children, arrived, send):
    def own(cols):
        return children[pick[0], :, cols]

    def far(cols):
        return arrived[:, cols]

    def step(pair, carry):
        for slot, child in ((0, own), (1, far)):
            send[pair, slot * BLK : (slot + 1) * BLK, :] = spread_tile(
                child, table[slot * 128 + 2 * pair], table[slot * 128 + 2 * pair + 1]
            )
        return carry

    lax.fori_loop(0, send.shape[0], step, 0, unroll=4)


def eliminate(work, fill):
    row = lax.broadcasted_iota(jnp.int32, (LEAF, HALF), 0)
    col = lax.broadcasted_iota(jnp.int32, (LEAF, HALF), 1)

    def spread(value, index):
        return jnp.broadcast_to(value[index : index + 1, :], (LEAF, HALF))

    def columns(value, base):
        return [jnp.broadcast_to(value[:, base + c : base + c + 1], (LEAF, HALF)) for c in range(LEAF)]

    left = work[:LEAF, :HALF]
    right = work[:LEAF, HALF:]
    wide = columns(left, 0)
    for base in range(0, HALF, LEAF):
        fill()
        more = base + LEAF < HALF
        if more:
            next_left = work[base + LEAF : base + 2 * LEAF, :HALF]
            next_right = work[base + LEAF : base + 2 * LEAF, HALF:]
            cross = columns(next_left, base)
        pivots = jnp.ones((LEAF, HALF), F32)
        for j in range(0, LEAF, 2):
            c0, c1 = wide[j], wide[j + 1]
            a, b, c = spread(c0, j), spread(c0, j + 1), spread(c1, j + 1)
            scale = 1.0 / (a * c - b * b)
            below = row > j + 1
            m0 = jnp.where(below, c0 * c - c1 * b, 0.0) * scale
            m1 = jnp.where(below, c1 * a - c0 * b, 0.0) * scale
            l0, l1 = spread(left, j), spread(left, j + 1)
            r0, r1 = spread(right, j), spread(right, j + 1)
            for k in range(j + 2, LEAF):
                wide[k] = wide[k] - (m0 * spread(c0, k) + m1 * spread(c1, k))
            if more:
                d0, d1 = cross[j], cross[j + 1]
                n0 = (d0 * c - d1 * b) * scale
                n1 = (d1 * a - d0 * b) * scale
                for k in range(j + 2, LEAF):
                    cross[k] = cross[k] - (n0 * spread(c0, k) + n1 * spread(c1, k))
                next_left = next_left - (n0 * l0 + n1 * l1)
                next_right = next_right - (n0 * r0 + n1 * r1)
            ratio = b / a
            m0 = jnp.where(row == j + 1, ratio, m0)
            pivots = jnp.where(row == j, a, jnp.where(row == j + 1, c - b * ratio, pivots))
            left = left - (m0 * l0 + m1 * l1)
            right = right - (m0 * r0 + m1 * r1)
        unit = lax.rsqrt(pivots)
        unit = unit * (1.5 - 0.5 * pivots * unit * unit)
        upper = jnp.where(col >= row + base, left * unit, 0.0)
        right = right * unit
        work[base : base + LEAF, :HALF] = upper
        work[base : base + LEAF, HALF:] = right
        if base + 2 * LEAF < HALF:
            beyond = upper.T[base + 2 * LEAF :]
            both = jnp.concatenate([upper, right], axis=1)
            product = exact_dot(beyond, both, 1, 0)
            work[base + 2 * LEAF :, :] = work[base + 2 * LEAF :, :] - product
        if more:
            left, right = next_left, next_right
            wide = columns(left, base + LEAF)


def exact_dot(left, right, left_dim, right_dim):
    return lax.dot_general(
        left,
        right,
        (((left_dim,), (right_dim,)), ((), ())),
        preferred_element_type=F32,
        precision=lax.Precision.HIGHEST,
    )


def pivot(block, work, fill):
    square = lax.broadcasted_iota(jnp.int32, (HALF, HALF), 0) == lax.broadcasted_iota(jnp.int32, (HALF, HALF), 1)
    eye = jnp.where(square, 1.0, 0.0)
    zero = jnp.zeros((HALF, HALF), F32)
    work[:, :HALF] = block[:HALF, :HALF]
    work[:, HALF:] = eye
    eliminate(work, fill)
    g11 = work[:, :HALF].T
    h11 = work[:, HALF:]
    g21 = exact_dot(block[HALF:, :HALF], h11, 1, 1)
    work[:, :HALF] = block[HALF:, HALF:] - exact_dot(g21, g21, 1, 1)
    work[:, HALF:] = eye
    eliminate(work, fill)
    g22 = work[:, :HALF].T
    h22 = work[:, HALF:]
    h21 = -exact_dot(h22, exact_dot(g21, h11, 1, 0), 1, 0)
    lower = jnp.concatenate([jnp.concatenate([g11, zero], 1), jnp.concatenate([g21, g22], 1)], 0)
    inverse = jnp.concatenate([jnp.concatenate([h11, zero], 1), jnp.concatenate([h21, h22], 1)], 0)
    return lower, inverse


def assemble_kernel(table, place, received, diag, base):
    device, active = place[0], place[1]
    cols = device * ROWS + lax.broadcasted_iota(jnp.int32, (BLK, ROWS), 1)

    def step(block, carry):
        total = None
        for slot in range(2):
            source = table[slot * 128 + block]
            part = received[jnp.maximum(source, 0), slot * BLK : (slot + 1) * BLK, :].astype(F32)
            part = jnp.where(source >= 0, part, 0.0)
            total = part if total is None else total + part
        rows = block * BLK + lax.broadcasted_iota(jnp.int32, (BLK, ROWS), 0)
        on = rows == cols
        total = total + jnp.where(on, diag[...], 0.0)
        outside = (rows >= active) | (cols >= active)
        total = jnp.where(outside, jnp.where(on, 1.0, 0.0), total)
        base[pl.ds(pl.multiple_of(block * BLK, BLK), BLK), :] = total.astype(BF16)
        return carry

    lax.fori_loop(0, base.shape[0] // BLK, step, 0, unroll=4)


def front_kernel(table, place, gathered, base, top_diag, out, panels, factor, trail, matrix, top, inverse, work, sems):
    device = place[0]
    start = pl.multiple_of(device * ROWS, ROWS)
    count = TOP // BLK
    jobs = 2 * (HALF // LEAF)
    rows = factor.shape[0] // jobs
    early = pltpu.make_async_copy(gathered.at[:count], panels.at[:count], sems.at[0])
    late = pltpu.make_async_copy(gathered.at[count:], panels.at[count:], sems.at[1])
    early.start()
    late.start()

    def row_block(block):
        total = None
        for slot in range(2):
            source = table[slot * 128 + block]
            part = panels[jnp.maximum(source, 0), slot * BLK : (slot + 1) * BLK, :].astype(F32)
            part = jnp.where(source >= 0, part, 0.0)
            total = part if total is None else total + part
        return total

    def gather_rows(job):
        if job == 0:
            late.wait()
        for block in range(job * rows // BLK, (job + 1) * rows // BLK):
            factor[block * BLK : (block + 1) * BLK, :] = row_block(block).astype(BF16)

    def solved_rows(panel, step):
        return (dot_nt(panel, inverse[step, 0]) + (dot_nt(panel, inverse[step, 1]) + dot_nt(panel, inverse[step, 2]))).astype(BF16)

    def solve_rows(step, job):
        spot = slice(job * rows, (job + 1) * rows)
        a, e = step * PW, (step + 1) * PW
        solved = solved_rows(factor[spot, a:e], step)
        factor[spot, a:e] = solved
        for after in range(step + 1, PANELS):
            b0, b1 = after * PW, (after + 1) * PW
            factor[spot, b0:b1] = (factor[spot, b0:b1].astype(F32) - dot_nt(solved, top[b0:b1, a:e])).astype(BF16)

    def update_rows(job):
        spot = slice(job * rows, (job + 1) * rows)
        own = factor[pl.ds(start, ROWS), :PW]
        trail[spot, :] = (base[spot, :].astype(F32) - dot_nt(factor[spot, :PW], own)).astype(BF16)

    early.wait()
    for block in range(count):
        on = lax.broadcasted_iota(jnp.int32, (BLK, TOP), 0) + block * BLK == lax.broadcasted_iota(
            jnp.int32, (BLK, TOP), 1
        )
        total = row_block(block) + jnp.where(on, top_diag[...], 0.0)
        matrix[block * BLK : (block + 1) * BLK, :] = rounded(total)
    top[...] = jnp.zeros_like(top)
    for step in range(PANELS):
        a, e = step * PW, (step + 1) * PW
        waiting = list(range(jobs))

        def fill(step=step, waiting=waiting):
            job = waiting.pop(0)
            if step == 0:
                gather_rows(job)
            else:
                solve_rows(step - 1, job)
                if step == PANELS - 1:
                    update_rows(job)

        lower, inner = pivot(matrix[a:e, a:e], work, fill)
        parts = split3(inner)
        for number in range(3):
            inverse[step, number] = parts[number]
        top[a:e, a:e] = lower.astype(BF16)
        if e < TOP:
            solved = solved_rows(matrix[e:, a:e].astype(BF16), step)
            top[e:, a:e] = solved
            matrix[e:, e:] = rounded(matrix[e:, e:] - dot_nt(solved, solved))

    last = TOP - PW
    mine = jnp.concatenate(
        [factor[pl.ds(start, ROWS), :last], solved_rows(factor[pl.ds(start, ROWS), last:], PANELS - 1)], axis=1
    )
    leading = device < TOP // ROWS
    own = jnp.where(leading, top[pl.ds(pl.multiple_of(jnp.minimum(start, TOP - ROWS), ROWS), ROWS), :], mine)

    def update(chunk, carry):
        spot = pl.ds(pl.multiple_of(chunk * CHUNK, CHUNK), CHUNK)
        tile = trail[spot, :].astype(F32)
        for step in range(1, PANELS):
            a, e = step * PW, (step + 1) * PW
            part = factor[spot, a:e]
            if e == TOP:
                part = solved_rows(part, step)
            tile = rounded(tile - dot_nt(part, own[:, a:e]))
        tile = jnp.where(leading, 0.0, tile)
        out[:, spot] = tile.T.astype(BF16)
        return carry

    lax.fori_loop(0, factor.shape[0] // CHUNK, update, 0)
    out[:, :TOP] = own


def body(front_diag, children, parent, front_blocks, child_blocks, row_map):
    leaf = lax.axis_index("leaf")
    grid = lax.axis_index("grid")
    devices = lax.axis_size("grid")
    front_order = front_diag.shape[1] * devices
    smem = pl.BlockSpec(memory_space=pltpu.SMEM)
    vmem = pl.BlockSpec(memory_space=pltpu.VMEM)
    anywhere = pl.BlockSpec(memory_space=pl.ANY)
    params = pltpu.CompilerParams(vmem_limit_bytes=VMEM_LIMIT)
    small = pltpu.CompilerParams(vmem_limit_bytes=16 * 1024 * 1024)

    narrow = children[:, :, :TOP]
    panel = pl.pallas_call(
        panel_kernel,
        out_shape=jax.ShapeDtypeStruct((2 * BLK, TOP), BF16),
        in_specs=[smem, smem, smem, smem, vmem, vmem],
        out_specs=vmem,
        compiler_params=small,
    )(leaf.astype(jnp.int32).reshape(1), parent, child_blocks, row_map, narrow, swapped(narrow))
    gathered = lax.all_gather(panel, "grid", axis=0, tiled=False)

    children, parent, panel = lax.optimization_barrier((children, parent, panel))
    first_own = 2 * leaf
    first_far = 2 * jnp.bitwise_xor(leaf, 1)
    own_slot = jnp.where(parent[first_own] == leaf, 0, 1).astype(jnp.int32)
    far_slot = jnp.where(parent[first_far] == leaf, 0, 1).astype(jnp.int32)
    arrived = swapped(lax.dynamic_index_in_dim(children, 1 - own_slot, 0, keepdims=False))
    ids = jnp.stack([first_own + own_slot, first_far + far_slot])
    maps = row_map[ids]
    numbers = jnp.arange(maps.shape[1], dtype=jnp.int32)
    live = numbers[None, :] < child_blocks[ids][:, None]
    hit = (maps[:, :, None] == jnp.arange(front_order // BLK)[None, None, :]) & live[:, :, None]
    table = jnp.max(jnp.where(hit, numbers[None, :, None], -1), axis=1).reshape(-1)
    send = pl.pallas_call(
        pack_kernel,
        out_shape=jax.ShapeDtypeStruct((devices, SENT, 128), BF16),
        in_specs=[smem, smem, vmem, vmem],
        out_specs=vmem,
        compiler_params=small,
    )(table, own_slot.reshape(1), children, arrived)
    received = lax.all_to_all(send, "grid", 0, 0, tiled=True)
    received, own_diag = lax.optimization_barrier((received, front_diag))
    copies = jnp.broadcast_to(own_diag, (devices, ROWS))
    top_diag = lax.all_to_all(copies, "grid", 0, 0, tiled=True)[: TOP // ROWS].reshape(1, TOP)
    place = jnp.stack([grid, front_blocks[leaf] * BLK]).astype(jnp.int32)
    base = pl.pallas_call(
        assemble_kernel,
        out_shape=jax.ShapeDtypeStruct((front_order, ROWS), BF16),
        in_specs=[smem, smem, vmem, vmem],
        out_specs=vmem,
        compiler_params=small,
    )(table, place, received, front_diag)
    factor = pl.pallas_call(
        front_kernel,
        out_shape=jax.ShapeDtypeStruct((ROWS, front_order), BF16),
        in_specs=[smem, smem, anywhere, vmem, vmem],
        out_specs=vmem,
        scratch_shapes=[
            pltpu.VMEM((devices, 2 * BLK, TOP), BF16),
            pltpu.VMEM((front_order, TOP), BF16),
            pltpu.VMEM((front_order, ROWS), BF16),
            pltpu.VMEM((TOP, TOP), F32),
            pltpu.VMEM((TOP, TOP), BF16),
            pltpu.VMEM((PANELS, 3, PW, PW), BF16),
            pltpu.VMEM((HALF, 2 * HALF), F32),
            pltpu.SemaphoreType.DMA((2,)),
        ],
        compiler_params=params,
    )(table, place, gathered, base, top_diag)
    return factor[None]


def solution(mesh):
    in_specs = (P("leaf", "grid"), P("leaf", "grid", None), P(), P(), P(), P())
    return jax.shard_map(body, mesh=mesh, in_specs=in_specs, out_specs=P("leaf", "grid", None), check_vma=False)
```
